32 devices in a mesh: seq: 4 (over y, x), req: 8 (over z, core).
Axes of the slice: x: 2, y: 2, z: 4, core: 2. Of those that a mesh axis runs over, the one named last changes fastest.
Arguments:
- hidden_in: bfloat16 [16, 256, 8192], P('req', 'seq'), may hold values from -6 to 6
- q_base: bfloat16 [16, 256, 1024], P('req', 'seq'), may hold values from -12 to 12
- kv_base: bfloat16 [16, 256, 256], P('req', 'seq'), may hold values from -6 to 6
- cache_kv: bfloat16 [16, 1024, 256], P('req', 'seq'), may hold values from -6 to 6
- req_adapter: int32 [16], replicated, may hold values from 0 to 7
- slot_of_adapter: int32 [8], replicated, may hold values from 0 to 7, each once
- down_panels: bfloat16 [8, 8192, 192], P('req', 'seq'), may hold values from -0.0625 to 0.0625
- up_panels: bfloat16 [8, 64, 2304], P('req', 'seq'), may hold values from -0.75 to 0.75
Outputs:
- attn_out: bfloat16 [16, 256, 1024], P('req', 'seq')
- o_low: float32 [16, 256, 64], P('req', 'seq')
- new_kv: bfloat16 [16, 256, 256], P('req', 'seq')
The draws below stay inside these ranges and needn't reach their ends.
Inputs may be any that keep to these rules, and one draw needn't show every extreme that they name: `req_adapter`: several requests may name the same adapter. `slot_of_adapter`: each adapter has its own slot.
All inputs are finite; a program needn't handle non-finite values.
Results may differ from the reference program's by a relative error of at most 0.012.
The reference program's roundings to bfloat16 on the way count: a program that leaves them out, or rounds other values in their place, can miss the bound.
Values may be sent and summed in bfloat16 or wider, within the bound.
A program may use at most 64 MiB of HBM per device.

```python
import math
import jax
import jax.numpy as jnp
import numpy as np
from jax import lax

D = 8192
HD = 128
HQ = 8
R = 64
REQS = 16
SPAN = 256
CTX = 1024
NADAPT = 8
QW = 1024
UPW = 2304


def draw_q_base(key, part):
    shape = (REQS, SPAN, HQ * HD)
    base = jnp.clip(jax.random.normal(jax.random.fold_in(key, 1), shape, jnp.float32), -6.0, 6.0)
    return base.astype(jnp.bfloat16)


def draw_cache_kv(key, part):
    shape = (REQS, CTX, 2 * HD)
    base = jnp.clip(jax.random.normal(jax.random.fold_in(key, 2), shape, jnp.float32), -6.0, 6.0)
    return base.astype(jnp.bfloat16)


def place_ends(values, key, least, top_value):
    extent = values.shape
    spot = [jax.random.randint(jax.random.fold_in(key, axis), (), 0, extent[axis]) for axis in range(len(extent))]
    values = values.at[tuple(spot)].set(least)
    longest = extent.index(max(extent))
    spot[longest] = (spot[longest] + 1) % extent[longest]
    return values.at[tuple(spot)].set(top_value)


def shard_levels(own_key, dims, split, least, top_value):
    loudness = 1.0
    for dim, parts in split:
        steps = jax.random.uniform(jax.random.fold_in(jax.random.fold_in(own_key, 6), dim), (parts,), jnp.float32, least / len(split), top_value / len(split))
        loudness = loudness * jnp.repeat(jnp.exp(steps), dims[dim] // parts).reshape((-1,) + (1,) * (len(dims) - 1 - dim))
    return loudness


def rank_table(number_of, lean):
    portions = [(1 << 20) // math.isqrt(rank ** lean) + 1 for rank in range(1, number_of + 1)]
    spread = 1 + sum(portions) // (1 << 30)
    return np.cumsum(np.array([max(1, weight // spread) for weight in portions]))


def ranked_ids(key, shape, amount, slope):
    listing = rank_table(amount, slope)
    pick = jax.random.randint(jax.random.fold_in(key, 1), shape, 0, int(listing[amount - 1]))
    grade = jnp.searchsorted(jnp.asarray(listing, jnp.int32), pick, side="right")
    return jax.random.permutation(jax.random.fold_in(key, 2), amount)[grade].astype(jnp.int32)


def normal_values(own_key, extent, spread, most, pieces=(), kind=jnp.bfloat16):
    factor_of = shard_levels(own_key, extent, pieces, -0.22, 0.18) if pieces else 1.0
    array = jax.random.normal(own_key, extent, jnp.float32) * spread * factor_of
    return jnp.minimum(jnp.maximum(array, -most), most).astype(kind)


def setup_inputs(seed: int = 0) -> dict:
    splits = jax.random.split(jax.random.key(seed), 9)
    hidden_in = normal_values(splits[0], (REQS, SPAN, D), 1.0, 6.0, ((0, 8), (1, 4)))
    q_base = draw_q_base(jax.random.fold_in(splits[8], 71), 0)
    kv_base = normal_values(splits[2], (REQS, SPAN, 2 * HD), 1.0, 6.0, ((0, 8), (1, 4)))
    cache_kv = draw_cache_kv(jax.random.fold_in(splits[8], 71), 0)
    req_adapter = place_ends(ranked_ids(splits[4], (REQS,), NADAPT, 2), jax.random.fold_in(splits[4], 3), 0, NADAPT - 1).astype(jnp.int32)
    slot_of_adapter = jax.random.permutation(splits[5], NADAPT).astype(jnp.int32)
    down_panels = normal_values(splits[6], (NADAPT, D, 3 * R), D ** -0.5, 0.0625, ((0, 8), (1, 4)))
    up_panels = normal_values(splits[7], (NADAPT, R, UPW), R ** -0.5, 0.75, ((0, 8), (1, 4)))
    return dict(hidden_in=hidden_in, q_base=q_base, kv_base=kv_base, cache_kv=cache_kv, req_adapter=req_adapter, slot_of_adapter=slot_of_adapter, down_panels=down_panels, up_panels=up_panels)


def rotate(vectors, positions):
    half_dim = vectors.shape[-1] // 2
    inverse = 500000.0 ** (-jnp.arange(half_dim, dtype=jnp.float32) / half_dim)
    angles = positions.astype(jnp.float32)[:, None] * inverse[None, :]
    cosine = jnp.cos(angles)[:, None, :]
    sine_part = jnp.sin(angles)[:, None, :]
    first_half = vectors[..., :half_dim]
    second_half = vectors[..., half_dim:]
    return jnp.concatenate([first_half * cosine - second_half * sine_part, second_half * cosine + first_half * sine_part], axis=-1)


def reference(hidden_in, q_base, kv_base, cache_kv, req_adapter, slot_of_adapter, down_panels, up_panels):
    slots = jnp.take(slot_of_adapter, req_adapter).astype(jnp.int32)

    def per_request(inputs):
        hidden, query_base, key_value, cached, slot_index = inputs
        down_panel = down_panels[slot_index]
        up_panel = up_panels[slot_index]
        low_rank = jnp.dot(hidden, down_panel, preferred_element_type=jnp.float32).astype(jnp.bfloat16)
        delta_q = jnp.dot(low_rank[:, :R], up_panel[:, :QW], preferred_element_type=jnp.float32)
        delta_k = jnp.dot(low_rank[:, R:2 * R], up_panel[:, QW:QW + HD], preferred_element_type=jnp.float32)
        delta_v = jnp.dot(low_rank[:, 2 * R:3 * R], up_panel[:, QW + HD:QW + 2 * HD], preferred_element_type=jnp.float32)
        positions = CTX + jnp.arange(SPAN, dtype=jnp.int32)
        queries = rotate((query_base.astype(jnp.float32) + delta_q).reshape(SPAN, HQ, HD), positions).astype(jnp.bfloat16)
        keys_new = rotate((key_value[:, :HD].astype(jnp.float32) + delta_k)[:, None, :], positions)[:, 0, :]
        values_new = key_value[:, HD:].astype(jnp.float32) + delta_v
        fresh_kv = jnp.concatenate([keys_new, values_new], axis=1).astype(jnp.bfloat16)
        all_keys = jnp.concatenate([cached[:, :HD], fresh_kv[:, :HD]], axis=0).astype(jnp.float32)
        all_values = jnp.concatenate([cached[:, HD:], fresh_kv[:, HD:]], axis=0).astype(jnp.float32)
        scores = jnp.einsum("thd,kd->htk", queries.astype(jnp.float32), all_keys) * (HD ** -0.5)
        key_index = jnp.arange(CTX + SPAN, dtype=jnp.int32)
        query_index = jnp.arange(SPAN, dtype=jnp.int32)
        visible = (key_index[None, :] < CTX) | ((key_index[None, :] - CTX) <= query_index[:, None])
        scores = jnp.where(visible[None], scores, -1e30)
        largest = jnp.max(scores, axis=-1, keepdims=True)
        weights = jnp.where(visible[None], jnp.exp(scores - largest), 0.0)
        denom = jnp.sum(weights, axis=-1)
        rounded = lax.optimization_barrier(weights.astype(jnp.bfloat16))
        mixed = jnp.einsum("htk,kd->thd", rounded.astype(jnp.float32), all_values)
        mixed = mixed / jnp.transpose(denom)[:, :, None]
        attention = mixed.reshape(SPAN, QW).astype(jnp.bfloat16)
        output_low = jnp.dot(attention, jnp.transpose(up_panel[:, QW + 2 * HD:]), preferred_element_type=jnp.float32)
        return attention, output_low, fresh_kv

    attn_out, o_low, new_kv = lax.map(per_request, (hidden_in, q_base, kv_base, cache_kv, slots))
    return (attn_out, o_low, new_kv)
```

```python
import functools

import jax
import jax.numpy as jnp
from jax import lax
from jax.experimental import pallas as pl
from jax.experimental.pallas import tpu as pltpu
from jax.sharding import PartitionSpec as P

masked_score = -1e30
MESH = pl.DeviceIdType.MESH


def rotate(vectors, positions):
    half_dim = vectors.shape[-1] // 2
    inverse = 500000.0 ** (-jnp.arange(half_dim, dtype=jnp.float32) / half_dim)
    angles = positions.astype(jnp.float32)[:, None] * inverse[None, :]
    cosine = jnp.cos(angles)[:, None, :]
    sine_part = jnp.sin(angles)[:, None, :]
    first_half = vectors[..., :half_dim]
    second_half = vectors[..., half_dim:]
    return jnp.concatenate(
        [
            first_half * cosine - second_half * sine_part,
            second_half * cosine + first_half * sine_part,
        ],
        axis=-1,
    )


def on_device(
    hidden_in, q_base, kv_base, cache_kv, req_adapter, slot_of_adapter, down_panels, up_panels
):
    requests, seg_rows, model_width = hidden_in.shape
    head_dim = kv_base.shape[2] // 2
    q_width = q_base.shape[2]
    head_count = q_width // head_dim
    rank_all = down_panels.shape[2]
    rank_size = rank_all // 3
    pre_rows = cache_kv.shape[1]
    seq_count = lax.axis_size("seq")
    seq_pos = lax.axis_index("seq")
    req_pos = lax.axis_index("req")
    context = pre_rows * seq_count
    my_adapters = lax.dynamic_slice_in_dim(req_adapter, req_pos * requests, requests)
    wanted = jnp.take(slot_of_adapter, my_adapters)
    pieces = (
        lax.all_gather(down_panels, "req", axis=0, tiled=True),
        lax.all_gather(up_panels, "req", axis=0, tiled=True),
    )
    slot_ids = jnp.arange(pieces[0].shape[0], dtype=jnp.int32)
    onehot = (wanted[:, None] == slot_ids[None, :]).astype(jnp.bfloat16)
    down_part = jnp.einsum("js,snc->jnc", onehot, pieces[0], preferred_element_type=jnp.float32)
    up_part = jnp.einsum("js,snc->jnc", onehot, pieces[1], preferred_element_type=jnp.float32)
    down_sel = down_part
    up_sel = up_part
    down_sel = down_sel.astype(jnp.bfloat16)
    up_sel = up_sel.astype(jnp.bfloat16)
    up_full = lax.all_gather(up_sel, "seq", axis=1, tiled=True)
    low_rank = jnp.einsum(
        "jtd,jdc->jtc",
        hidden_in,
        lax.all_gather(down_sel, "seq", axis=1, tiled=True),
        preferred_element_type=jnp.float32,
    )
    low_half = low_rank.astype(jnp.bfloat16)
    delta_q = jnp.einsum(
        "jtr,jrc->jtc",
        low_half[:, :, :rank_size],
        up_full[:, :, :q_width],
        preferred_element_type=jnp.float32,
    )
    delta_k = jnp.einsum(
        "jtr,jrc->jtc",
        low_half[:, :, rank_size : 2 * rank_size],
        up_full[:, :, q_width : q_width + head_dim],
        preferred_element_type=jnp.float32,
    )
    delta_v = jnp.einsum(
        "jtr,jrc->jtc",
        low_half[:, :, 2 * rank_size :],
        up_full[:, :, q_width + head_dim : q_width + 2 * head_dim],
        preferred_element_type=jnp.float32,
    )
    query_index = seq_pos * seg_rows + jnp.arange(seg_rows, dtype=jnp.int32)
    positions = context + query_index
    queries = rotate(
        (q_base.astype(jnp.float32) + delta_q).reshape(requests, seg_rows, head_count, head_dim),
        positions,
    ).astype(jnp.bfloat16)
    keys_new = rotate(
        (kv_base[:, :, :head_dim].astype(jnp.float32) + delta_k)[:, :, None, :], positions
    )[:, :, 0, :]
    values_new = kv_base[:, :, head_dim:].astype(jnp.float32) + delta_v
    new_kv = jnp.concatenate([keys_new, values_new], axis=2).astype(jnp.bfloat16)
    local_kv = jnp.concatenate([cache_kv, new_kv], axis=1)
    kv_rows = pre_rows + seg_rows
    score_scale = head_dim ** (-0.5)

    def attend_block(state_now, key_block, first_row):
        running_max, running_sum, weighted = state_now
        key_part = key_block[:, :, :head_dim]
        value_part = key_block[:, :, head_dim:]
        scores = (
            jnp.einsum("jthd,jkd->jhtk", queries, key_part, preferred_element_type=jnp.float32)
            * score_scale
        )
        global_index = first_row + jnp.arange(key_block.shape[1], dtype=jnp.int32)
        owner_dev = global_index // kv_rows
        offset = global_index % kv_rows
        span_index = owner_dev * seg_rows + offset - pre_rows
        visible = (offset[None, :] < pre_rows) | (span_index[None, :] <= query_index[:, None])
        scores = jnp.where(visible[None, None], scores, masked_score)
        newest = jnp.maximum(running_max, jnp.max(scores, axis=-1))
        weights = jnp.where(visible[None, None], jnp.exp(scores - newest[..., None]), 0.0)
        factor = jnp.exp(running_max - newest)
        running_sum = running_sum * factor + jnp.sum(weights, axis=-1)
        weighted = weighted * factor[..., None] + jnp.einsum(
            "jhtk,jkd->jhtd",
            weights.astype(jnp.bfloat16),
            value_part,
            preferred_element_type=jnp.float32,
        )
        return (newest, running_sum, weighted)

    start_state = (
        jnp.full((requests, head_count, seg_rows), masked_score, jnp.float32),
        jnp.zeros((requests, head_count, seg_rows), jnp.float32),
        jnp.zeros((requests, head_count, seg_rows, head_dim), jnp.float32),
    )
    kv_piece = lax.all_gather(local_kv, "seq", axis=1, tiled=True)
    piece_rows = kv_piece.shape[1]

    def advance(block_number, state_inner):
        key_block = lax.dynamic_slice_in_dim(kv_piece, block_number * kv_rows, kv_rows, 1)
        return attend_block(state_inner, key_block, block_number * kv_rows)

    running_max, running_sum, weighted = lax.fori_loop(
        0, piece_rows // kv_rows, advance, start_state
    )
    mixed = weighted / running_sum[..., None]
    attn_out = (
        jnp.transpose(mixed, (0, 2, 1, 3)).reshape(requests, seg_rows, q_width).astype(jnp.bfloat16)
    )
    o_low = jnp.einsum(
        "jtc,jrc->jtr",
        attn_out,
        up_full[:, :, q_width + 2 * head_dim :],
        preferred_element_type=jnp.float32,
    )
    return (attn_out, o_low, new_kv)

def attend_kernel(
    z_count,
    req_adapter,
    slot_of_adapter,
    hidden_in,
    down_in,
    up_in,
    cache_in,
    q_base,
    kv_base,
    cos_in,
    sin_in,
    attn_out,
    o_low,
    new_kv,
    hid,
    down_all,
    up_all,
    up_sel,
    up_got,
    kv_all,
    kv_new,
    part,
    part_got,
    queries,
    acc,
    top,
    total,
    local_sem,
    hid_send,
    hid_recv,
    kv_send,
    kv_recv,
    up_send,
    up_recv,
    part_send,
    part_recv,
    new_send,
    new_recv,
    z_send,
    z_recv,
    mate_send,
    mate_recv,
):
    requests, rows, _ = q_base.shape
    seq_count, _, _, depth = hid.shape
    head_dim = kv_base.shape[2] // 2
    q_width = q_base.shape[2]
    head_count = q_width // head_dim
    rank = head_dim // 2
    pre_rows = cache_in.shape[1]
    span = seq_count * rows
    seq = lax.axis_index("seq")
    req = lax.axis_index("req")
    z = req // 2
    core = req % 2
    mate = {"req": z * 2 + (1 - core)}
    ahead = {"req": req + 2}
    behind = {"req": req - 2}
    peers = [lax.rem(seq + k, seq_count) for k in range(seq_count)]

    def send(src, dst, s_sem, r_sem, target):
        return pltpu.make_async_remote_copy(
            src_ref=src,
            dst_ref=dst,
            send_sem=s_sem,
            recv_sem=r_sem,
            device_id=target,
            device_id_type=MESH,
        )

    local = [
        pltpu.make_async_copy(hidden_in.at[:, :, pl.ds(seq * depth, depth)], hid.at[seq], local_sem.at[0]),
        pltpu.make_async_copy(cache_in, kv_all.at[:, pl.ds(seq * pre_rows, pre_rows), :], local_sem.at[1]),
        pltpu.make_async_copy(down_in, down_all.at[req], local_sem.at[2]),
        pltpu.make_async_copy(up_in, up_all.at[req], local_sem.at[3]),
    ]
    for copy in local:
        copy.start()

    barrier = pltpu.get_barrier_semaphore()
    for k in range(1, seq_count):
        pl.semaphore_signal(barrier, inc=1, device_id={"seq": peers[k]}, device_id_type=MESH)
    pl.semaphore_signal(barrier, inc=1, device_id=mate, device_id_type=MESH)

    @pl.when(z > 0)
    def _():
        pl.semaphore_signal(barrier, inc=1, device_id=behind, device_id_type=MESH)

    @pl.when(z < z_count - 1)
    def _():
        pl.semaphore_signal(barrier, inc=1, device_id=ahead, device_id_type=MESH)

    ends = (z > 0).astype(jnp.int32) + (z < z_count - 1).astype(jnp.int32)
    pl.semaphore_wait(barrier, seq_count + ends)

    held = (up_all, down_all)
    own = (up_in, down_in)

    def along(way, step, kind, chip, src=None):
        slot = chip * 2 + core
        return send(
            held[kind].at[slot] if src is None else src,
            held[kind].at[slot],
            z_send.at[way, step, kind],
            z_recv.at[way, step, kind],
            ahead if way == 0 else behind,
        )

    def across(kind, chip, src=None):
        slot = chip * 2 + core
        return send(
            held[kind].at[slot] if src is None else src,
            held[kind].at[slot],
            mate_send.at[kind, chip],
            mate_recv.at[kind, chip],
            mate,
        )

    def can_send(way, step):
        if way == 0:
            return (z < z_count - 1) & (z - step >= 0)
        return (z > 0) & (z + step <= z_count - 1)

    def can_get(way, step):
        return z - 1 - step >= 0 if way == 0 else z + 1 + step <= z_count - 1

    def passed(way, step):
        return z - step if way == 0 else z + step

    for way in range(2):

        @pl.when(can_send(way, 0))
        def _(way=way):
            for kind in range(2):
                along(way, 0, kind, z, own[kind]).start()

    for kind in range(2):
        across(kind, z, own[kind]).start()

    def hid_copy(k):
        return send(
            hidden_in.at[:, :, pl.ds(peers[k] * depth, depth)],
            hid.at[seq],
            hid_send.at[k],
            hid_recv.at[k],
            {"seq": peers[k]},
        )

    def kv_copy(k):
        return send(
            cache_in,
            kv_all.at[:, pl.ds(seq * pre_rows, pre_rows), :],
            kv_send.at[k],
            kv_recv.at[k],
            {"seq": peers[k]},
        )

    def up_copy(k):
        return send(up_sel, up_got.at[seq], up_send.at[k], up_recv.at[k], {"seq": peers[k]})

    def part_copy(k):
        return send(
            part.at[peers[k]], part_got.at[k], part_send.at[k], part_recv.at[k], {"seq": peers[k]}
        )

    def new_copy(k):
        here = kv_new.at[:, pl.ds(seq * rows, rows), :]
        return send(here, here, new_send.at[k], new_recv.at[k], {"seq": peers[k]})

    others = range(1, seq_count)
    for k in others:
        hid_copy(k).start()
    for k in others:
        kv_copy(k).start()

    def relay(step, kind):
        for way in range(2):

            @pl.when(can_get(way, step))
            def _(way=way):
                chip = passed(way, step + 1)
                along(way, step, kind, chip).wait_recv()
                across(kind, chip).start()

            if step + 1 < z_count - 1:

                @pl.when(can_send(way, step + 1))
                def _(way=way):
                    along(way, step + 1, kind, passed(way, step + 1)).start()

    for step in range(z_count - 1):
        relay(step, 0)
        if step < z_count - 2:
            relay(step, 1)

    wanted = [slot_of_adapter[req_adapter[req * requests + j]] for j in range(requests)]
    local[3].wait()
    for chip in range(z_count):
        across(0, chip).wait_recv()
    for j in range(requests):
        up_sel[j] = up_all[wanted[j]]
    for k in others:
        up_copy(k).start()
    relay(z_count - 2, 1)
    for j in range(requests):
        up_got[seq, j] = up_sel[j]
    for copy in local[:3]:
        copy.wait()
    for k in others:
        hid_copy(k).wait_recv()
    for chip in range(z_count):
        across(1, chip).wait_recv()

    contract = (((1,), (1,)), ((), ()))
    thin = []
    for j in range(requests):
        h = hid[:, j].reshape(span, depth)
        thick = lax.dot_general(h, down_all[wanted[j]], contract, preferred_element_type=jnp.float32)
        thin.append(thick[:, head_dim:])
        for s in range(seq_count):
            part[s, j * rows : (j + 1) * rows, :] = thick[s * rows : (s + 1) * rows, :head_dim]
    joined = jnp.concatenate(thin, axis=1)
    for s in range(seq_count):
        part[s, requests * rows :, :] = joined[s * rows : (s + 1) * rows]
    for k in others:
        part_copy(k).start()

    for k in others:
        up_copy(k).wait_recv()
    for k in others:
        part_copy(k).wait_recv()
    low = part[seq]
    for k in others:
        low = low + part_got[k]
    low = low.astype(jnp.bfloat16)
    cosine = cos_in[...]
    sine = sin_in[...]

    def rotated(u):
        return u * cosine + pltpu.roll(u, rank, 1) * sine

    ups = [up_got[:, j].reshape(rank, up_got.shape[3]) for j in range(requests)]
    for j in range(requests):
        low_k = low[j * rows : (j + 1) * rows, rank:]
        low_v = low[requests * rows :, j * rank : (j + 1) * rank]
        up = ups[j]
        delta_k = jnp.dot(low_k, up[:, q_width : q_width + head_dim], preferred_element_type=jnp.float32)
        delta_v = jnp.dot(
            low_v,
            up[:, q_width + head_dim : q_width + 2 * head_dim],
            preferred_element_type=jnp.float32,
        )
        base = kv_base[j].astype(jnp.float32)
        key = rotated(base[:, :head_dim] + delta_k).astype(jnp.bfloat16)
        value = (base[:, head_dim:] + delta_v).astype(jnp.bfloat16)
        fresh = jnp.concatenate([key, value], axis=1)
        new_kv[j] = fresh
        kv_new[j, pl.ds(seq * rows, rows), :] = fresh
    for k in others:
        new_copy(k).start()

    for j in range(requests):
        low_q = low[j * rows : (j + 1) * rows, :rank]
        delta_q = jnp.dot(low_q, ups[j][:, :q_width], preferred_element_type=jnp.float32)
        for h in range(head_count):
            cols = slice(h * head_dim, (h + 1) * head_dim)
            u = q_base[j, :, cols].astype(jnp.float32) + delta_q[:, cols]
            queries[j, h * rows : (h + 1) * rows, :] = rotated(u).astype(jnp.bfloat16)

    for k in others:
        kv_copy(k).wait_recv()
    scale = head_dim ** (-0.5)
    group = 4 * rows
    for j in range(requests):
        for g in range(head_count * rows // group):
            at = slice(g * group, (g + 1) * group)
            scores = (
                lax.dot_general(
                    queries[j, at, :],
                    kv_all[j, :, :head_dim],
                    contract,
                    preferred_element_type=jnp.float32,
                )
                * scale
            )
            m = jnp.max(scores, axis=1, keepdims=True)
            w = jnp.exp(scores - m)
            top[j, at, :] = jnp.broadcast_to(m, (group, head_dim))
            total[j, at, :] = jnp.broadcast_to(jnp.sum(w, axis=1, keepdims=True), (group, head_dim))
            acc[j, at, :] = jnp.dot(
                w.astype(jnp.bfloat16), kv_all[j, :, head_dim:], preferred_element_type=jnp.float32
            )

    for k in others:
        new_copy(k).wait_recv()
    token = lax.rem(lax.broadcasted_iota(jnp.int32, (group, span), 0), rows) + seq * rows
    visible = lax.broadcasted_iota(jnp.int32, (group, span), 1) <= token
    for j in range(requests):
        heads = []
        for g in range(head_count * rows // group):
            at = slice(g * group, (g + 1) * group)
            scores = (
                lax.dot_general(
                    queries[j, at, :],
                    kv_new[j, :, :head_dim],
                    contract,
                    preferred_element_type=jnp.float32,
                )
                * scale
            )
            scores = jnp.where(visible, scores, masked_score)
            old = top[j, at, :]
            m = jnp.maximum(old, jnp.max(scores, axis=1, keepdims=True))
            w = jnp.exp(scores - m[:, :1])
            factor = jnp.exp(old - m)
            denom = total[j, at, :] * factor + jnp.sum(w, axis=1, keepdims=True)
            mixed = acc[j, at, :] * factor + jnp.dot(
                w.astype(jnp.bfloat16), kv_new[j, :, head_dim:], preferred_element_type=jnp.float32
            )
            mixed = (mixed / denom).astype(jnp.bfloat16)
            for i in range(group // rows):
                heads.append(mixed[i * rows : (i + 1) * rows])
        attention = jnp.concatenate(heads, axis=1)
        attn_out[j] = attention
        o_low[j] = lax.dot_general(
            attention, ups[j][:, q_width + 2 * head_dim :], contract, preferred_element_type=jnp.float32
        )

    for k in others:
        for copy in (hid_copy(k), kv_copy(k), up_copy(k), part_copy(k), new_copy(k)):
            copy.wait_send()
    for kind in range(2):
        for chip in range(z_count):
            across(kind, chip).wait_send()
        for way in range(2):
            for step in range(z_count - 1):

                @pl.when(can_send(way, step))
                def _(way=way, step=step, kind=kind):
                    along(way, step, kind, passed(way, step)).wait_send()


def fused(
    hidden_in, q_base, kv_base, cache_kv, req_adapter, slot_of_adapter, down_panels, up_panels
):
    requests, rows, _ = hidden_in.shape
    head_dim = kv_base.shape[2] // 2
    q_width = q_base.shape[2]
    pre_rows = cache_kv.shape[1]
    seq_count = lax.axis_size("seq")
    req_count = lax.axis_size("req")
    depth = down_panels.shape[1]
    rank_rows, up_width = up_panels.shape[1:]
    z_count = req_count // 2
    half_dim = head_dim // 2
    panel = down_panels[0].T
    positions = (
        pre_rows * seq_count
        + lax.axis_index("seq") * rows
        + jnp.arange(rows, dtype=jnp.int32)
    )
    inverse = 500000.0 ** (-jnp.arange(half_dim, dtype=jnp.float32) / half_dim)
    angles = positions.astype(jnp.float32)[:, None] * inverse[None, :]
    cosine = jnp.cos(angles)
    sine = jnp.sin(angles)
    cosine = jnp.concatenate([cosine, cosine], axis=1)
    sine = jnp.concatenate([-sine, sine], axis=1)
    span = seq_count * rows
    q_rows = q_width // head_dim * rows
    bf16, f32 = jnp.bfloat16, jnp.float32
    dma = pltpu.SemaphoreType.DMA
    smem = pl.BlockSpec(memory_space=pltpu.SMEM)
    vmem = pl.BlockSpec(memory_space=pltpu.VMEM)
    anywhere = pl.BlockSpec(memory_space=pltpu.HBM)
    return pl.pallas_call(
        functools.partial(attend_kernel, z_count),
        out_shape=(
            jax.ShapeDtypeStruct((requests, rows, q_width), bf16),
            jax.ShapeDtypeStruct((requests, rows, half_dim), f32),
            jax.ShapeDtypeStruct((requests, rows, 2 * head_dim), bf16),
        ),
        in_specs=[smem, smem, anywhere, anywhere, anywhere, anywhere, vmem, vmem, vmem, vmem],
        out_specs=(vmem, vmem, vmem),
        scratch_shapes=[
            pltpu.VMEM((seq_count, requests, rows, depth), bf16),
            pltpu.VMEM((req_count,) + panel.shape, bf16),
            pltpu.VMEM((req_count, rank_rows, up_width), bf16),
            pltpu.VMEM((requests, rank_rows, up_width), bf16),
            pltpu.VMEM((seq_count, requests, rank_rows, up_width), bf16),
            pltpu.VMEM((requests, seq_count * pre_rows, 2 * head_dim), bf16),
            pltpu.VMEM((requests, span, 2 * head_dim), bf16),
            pltpu.VMEM((seq_count, (requests + 1) * rows, head_dim), f32),
            pltpu.VMEM((seq_count, (requests + 1) * rows, head_dim), f32),
            pltpu.VMEM((requests, q_rows, head_dim), bf16),
            pltpu.VMEM((requests, q_rows, head_dim), f32),
            pltpu.VMEM((requests, q_rows, head_dim), f32),
            pltpu.VMEM((requests, q_rows, head_dim), f32),
            dma((4,)),
        ]
        + [dma((seq_count,))] * 10
        + [dma((2, z_count - 1, 2))] * 2
        + [dma((2, z_count))] * 2,
        compiler_params=pltpu.CompilerParams(
            collective_id=0, has_side_effects=True, vmem_limit_bytes=48 * 1024 * 1024
        ),
    )(
        req_adapter,
        slot_of_adapter,
        hidden_in,
        panel,
        up_panels[0],
        cache_kv,
        q_base,
        kv_base,
        cosine,
        sine,
    )


def fits(mesh):
    return mesh.shape["req"] % 2 == 0 and mesh.shape["seq"] <= 4


def solution(mesh):
    return jax.shard_map(
        fused if fits(mesh) else on_device,
        mesh=mesh,
        in_specs=(
            P("req", "seq", None),
            P("req", "seq", None),
            P("req", "seq", None),
            P("req", "seq", None),
            P(),
            P(),
            P("req", "seq", None),
            P("req", "seq", None),
        ),
        out_specs=(P("req", "seq", None), P("req", "seq", None), P("req", "seq", None)),
        check_vma=False,
    )
```

```python
import functools

import jax
import jax.numpy as jnp
from jax import lax
from jax.experimental import pallas as pl
from jax.experimental.pallas import tpu as pltpu
from jax.sharding import PartitionSpec as P

masked_score = -1e30
MESH = pl.DeviceIdType.MESH


def rotate(vectors, positions):
    half_dim = vectors.shape[-1] // 2
    inverse = 500000.0 ** (-jnp.arange(half_dim, dtype=jnp.float32) / half_dim)
    angles = positions.astype(jnp.float32)[:, None] * inverse[None, :]
    cosine = jnp.cos(angles)[:, None, :]
    sine_part = jnp.sin(angles)[:, None, :]
    first_half = vectors[..., :half_dim]
    second_half = vectors[..., half_dim:]
    return jnp.concatenate(
        [
            first_half * cosine - second_half * sine_part,
            second_half * cosine + first_half * sine_part,
        ],
        axis=-1,
    )


def on_device(
    hidden_in, q_base, kv_base, cache_kv, req_adapter, slot_of_adapter, down_panels, up_panels
):
    requests, seg_rows, model_width = hidden_in.shape
    head_dim = kv_base.shape[2] // 2
    q_width = q_base.shape[2]
    head_count = q_width // head_dim
    rank_all = down_panels.shape[2]
    rank_size = rank_all // 3
    pre_rows = cache_kv.shape[1]
    seq_count = lax.axis_size("seq")
    seq_pos = lax.axis_index("seq")
    req_pos = lax.axis_index("req")
    context = pre_rows * seq_count
    my_adapters = lax.dynamic_slice_in_dim(req_adapter, req_pos * requests, requests)
    wanted = jnp.take(slot_of_adapter, my_adapters)
    pieces = (
        lax.all_gather(down_panels, "req", axis=0, tiled=True),
        lax.all_gather(up_panels, "req", axis=0, tiled=True),
    )
    slot_ids = jnp.arange(pieces[0].shape[0], dtype=jnp.int32)
    onehot = (wanted[:, None] == slot_ids[None, :]).astype(jnp.bfloat16)
    down_part = jnp.einsum("js,snc->jnc", onehot, pieces[0], preferred_element_type=jnp.float32)
    up_part = jnp.einsum("js,snc->jnc", onehot, pieces[1], preferred_element_type=jnp.float32)
    down_sel = down_part
    up_sel = up_part
    down_sel = down_sel.astype(jnp.bfloat16)
    up_sel = up_sel.astype(jnp.bfloat16)
    up_full = lax.all_gather(up_sel, "seq", axis=1, tiled=True)
    low_rank = jnp.einsum(
        "jtd,jdc->jtc",
        hidden_in,
        lax.all_gather(down_sel, "seq", axis=1, tiled=True),
        preferred_element_type=jnp.float32,
    )
    low_half = low_rank.astype(jnp.bfloat16)
    delta_q = jnp.einsum(
        "jtr,jrc->jtc",
        low_half[:, :, :rank_size],
        up_full[:, :, :q_width],
        preferred_element_type=jnp.float32,
    )
    delta_k = jnp.einsum(
        "jtr,jrc->jtc",
        low_half[:, :, rank_size : 2 * rank_size],
        up_full[:, :, q_width : q_width + head_dim],
        preferred_element_type=jnp.float32,
    )
    delta_v = jnp.einsum(
        "jtr,jrc->jtc",
        low_half[:, :, 2 * rank_size :],
        up_full[:, :, q_width + head_dim : q_width + 2 * head_dim],
        preferred_element_type=jnp.float32,
    )
    query_index = seq_pos * seg_rows + jnp.arange(seg_rows, dtype=jnp.int32)
    positions = context + query_index
    queries = rotate(
        (q_base.astype(jnp.float32) + delta_q).reshape(requests, seg_rows, head_count, head_dim),
        positions,
    ).astype(jnp.bfloat16)
    keys_new = rotate(
        (kv_base[:, :, :head_dim].astype(jnp.float32) + delta_k)[:, :, None, :], positions
    )[:, :, 0, :]
    values_new = kv_base[:, :, head_dim:].astype(jnp.float32) + delta_v
    new_kv = jnp.concatenate([keys_new, values_new], axis=2).astype(jnp.bfloat16)
    local_kv = jnp.concatenate([cache_kv, new_kv], axis=1)
    kv_rows = pre_rows + seg_rows
    score_scale = head_dim ** (-0.5)

    def attend_block(state_now, key_block, first_row):
        running_max, running_sum, weighted = state_now
        key_part = key_block[:, :, :head_dim]
        value_part = key_block[:, :, head_dim:]
        scores = (
            jnp.einsum("jthd,jkd->jhtk", queries, key_part, preferred_element_type=jnp.float32)
            * score_scale
        )
        global_index = first_row + jnp.arange(key_block.shape[1], dtype=jnp.int32)
        owner_dev = global_index // kv_rows
        offset = global_index % kv_rows
        span_index = owner_dev * seg_rows + offset - pre_rows
        visible = (offset[None, :] < pre_rows) | (span_index[None, :] <= query_index[:, None])
        scores = jnp.where(visible[None, None], scores, masked_score)
        newest = jnp.maximum(running_max, jnp.max(scores, axis=-1))
        weights = jnp.where(visible[None, None], jnp.exp(scores - newest[..., None]), 0.0)
        factor = jnp.exp(running_max - newest)
        running_sum = running_sum * factor + jnp.sum(weights, axis=-1)
        weighted = weighted * factor[..., None] + jnp.einsum(
            "jhtk,jkd->jhtd",
            weights.astype(jnp.bfloat16),
            value_part,
            preferred_element_type=jnp.float32,
        )
        return (newest, running_sum, weighted)

    start_state = (
        jnp.full((requests, head_count, seg_rows), masked_score, jnp.float32),
        jnp.zeros((requests, head_count, seg_rows), jnp.float32),
        jnp.zeros((requests, head_count, seg_rows, head_dim), jnp.float32),
    )
    kv_piece = lax.all_gather(local_kv, "seq", axis=1, tiled=True)
    piece_rows = kv_piece.shape[1]

    def advance(block_number, state_inner):
        key_block = lax.dynamic_slice_in_dim(kv_piece, block_number * kv_rows, kv_rows, 1)
        return attend_block(state_inner, key_block, block_number * kv_rows)

    running_max, running_sum, weighted = lax.fori_loop(
        0, piece_rows // kv_rows, advance, start_state
    )
    mixed = weighted / running_sum[..., None]
    attn_out = (
        jnp.transpose(mixed, (0, 2, 1, 3)).reshape(requests, seg_rows, q_width).astype(jnp.bfloat16)
    )
    o_low = jnp.einsum(
        "jtc,jrc->jtr",
        attn_out,
        up_full[:, :, q_width + 2 * head_dim :],
        preferred_element_type=jnp.float32,
    )
    return (attn_out, o_low, new_kv)

def attend_kernel(
    z_count,
    req_adapter,
    slot_of_adapter,
    hidden_in,
    down_in,
    up_in,
    cache_in,
    q_base,
    kv_base,
    cos_in,
    sin_in,
    attn_out,
    o_low,
    new_kv,
    hid,
    down_all,
    down_end,
    up_all,
    up_sel,
    up_got,
    kv_all,
    kv_new,
    part,
    part_got,
    part_end,
    end_got,
    queries,
    acc,
    top,
    total,
    local_sem,
    hid_send,
    hid_recv,
    kv_send,
    kv_recv,
    up_send,
    up_recv,
    part_send,
    part_recv,
    end_send,
    end_recv,
    new_send,
    new_recv,
    z_send,
    z_recv,
    mate_send,
    mate_recv,
):
    requests, rows, _ = q_base.shape
    seq_count, _, _, depth = hid.shape
    head_dim = kv_base.shape[2] // 2
    q_width = q_base.shape[2]
    head_count = q_width // head_dim
    rank = head_dim // 2
    pre_rows = cache_in.shape[1]
    span = seq_count * rows
    seq = lax.axis_index("seq")
    req = lax.axis_index("req")
    z = req // 2
    core = req % 2
    mate = {"req": z * 2 + (1 - core)}
    ahead = {"req": req + 2}
    behind = {"req": req - 2}
    peers = [lax.rem(seq + k, seq_count) for k in range(seq_count)]

    def send(src, dst, s_sem, r_sem, target):
        return pltpu.make_async_remote_copy(
            src_ref=src,
            dst_ref=dst,
            send_sem=s_sem,
            recv_sem=r_sem,
            device_id=target,
            device_id_type=MESH,
        )

    held = (up_all, down_all, down_end)
    own = (up_in, down_in.at[pl.ds(0, head_dim)], down_in.at[pl.ds(head_dim, rank)])
    local = [
        pltpu.make_async_copy(hidden_in.at[:, :, pl.ds(seq * depth, depth)], hid.at[seq], local_sem.at[0]),
        pltpu.make_async_copy(cache_in, kv_all.at[:, pl.ds(seq * pre_rows, pre_rows), :], local_sem.at[1]),
        pltpu.make_async_copy(own[1], down_all.at[req], local_sem.at[2]),
        pltpu.make_async_copy(own[2], down_end.at[req], local_sem.at[3]),
        pltpu.make_async_copy(own[0], up_all.at[req], local_sem.at[4]),
    ]
    for copy in local:
        copy.start()

    barrier = pltpu.get_barrier_semaphore()
    for k in range(1, seq_count):
        pl.semaphore_signal(barrier, inc=1, device_id={"seq": peers[k]}, device_id_type=MESH)
    pl.semaphore_signal(barrier, inc=1, device_id=mate, device_id_type=MESH)

    @pl.when(z > 0)
    def _():
        pl.semaphore_signal(barrier, inc=1, device_id=behind, device_id_type=MESH)

    @pl.when(z < z_count - 1)
    def _():
        pl.semaphore_signal(barrier, inc=1, device_id=ahead, device_id_type=MESH)

    ends = (z > 0).astype(jnp.int32) + (z < z_count - 1).astype(jnp.int32)
    pl.semaphore_wait(barrier, seq_count + ends)

    def along(way, step, kind, chip, src=None):
        slot = chip * 2 + core
        return send(
            held[kind].at[slot] if src is None else src,
            held[kind].at[slot],
            z_send.at[way, step, kind],
            z_recv.at[way, step, kind],
            ahead if way == 0 else behind,
        )

    def across(kind, chip, src=None):
        slot = chip * 2 + core
        return send(
            held[kind].at[slot] if src is None else src,
            held[kind].at[slot],
            mate_send.at[kind, chip],
            mate_recv.at[kind, chip],
            mate,
        )

    def can_send(way, step):
        if way == 0:
            return (z < z_count - 1) & (z - step >= 0)
        return (z > 0) & (z + step <= z_count - 1)

    def can_get(way, step):
        return z - 1 - step >= 0 if way == 0 else z + 1 + step <= z_count - 1

    def passed(way, step):
        return z - step if way == 0 else z + step

    for way in range(2):

        @pl.when(can_send(way, 0))
        def _(way=way):
            for kind in range(3):
                along(way, 0, kind, z, own[kind]).start()

    for kind in range(3):
        across(kind, z, own[kind]).start()

    def hid_copy(k):
        return send(
            hidden_in.at[:, :, pl.ds(peers[k] * depth, depth)],
            hid.at[seq],
            hid_send.at[k],
            hid_recv.at[k],
            {"seq": peers[k]},
        )

    def kv_copy(k):
        return send(
            cache_in,
            kv_all.at[:, pl.ds(seq * pre_rows, pre_rows), :],
            kv_send.at[k],
            kv_recv.at[k],
            {"seq": peers[k]},
        )

    def up_copy(k):
        return send(up_sel, up_got.at[seq], up_send.at[k], up_recv.at[k], {"seq": peers[k]})

    def part_copy(k):
        return send(
            part.at[peers[k]], part_got.at[k], part_send.at[k], part_recv.at[k], {"seq": peers[k]}
        )

    def end_copy(k):
        return send(
            part_end.at[peers[k]], end_got.at[k], end_send.at[k], end_recv.at[k], {"seq": peers[k]}
        )

    def new_copy(k):
        here = kv_new.at[:, pl.ds(seq * rows, rows), :]
        return send(here, here, new_send.at[k], new_recv.at[k], {"seq": peers[k]})

    others = range(1, seq_count)
    for k in others:
        hid_copy(k).start()
    for k in others:
        kv_copy(k).start()

    def relay(step, kind):
        for way in range(2):

            @pl.when(can_get(way, step))
            def _(way=way):
                chip = passed(way, step + 1)
                along(way, step, kind, chip).wait_recv()
                across(kind, chip).start()

            if step + 1 < z_count - 1:

                @pl.when(can_send(way, step + 1))
                def _(way=way):
                    along(way, step + 1, kind, passed(way, step + 1)).start()

    for step in range(z_count - 1):
        relay(step, 0)
        if step < z_count - 2:
            relay(step, 1)
            relay(step, 2)

    wanted = [slot_of_adapter[req_adapter[req * requests + j]] for j in range(requests)]
    local[4].wait()
    for chip in range(z_count):
        across(0, chip).wait_recv()
    for j in range(requests):
        up_sel[j] = up_all[wanted[j]]
    for k in others:
        up_copy(k).start()
    relay(z_count - 2, 1)
    for j in range(requests):
        up_got[seq, j] = up_sel[j]
    for copy in local[:4]:
        copy.wait()
    for k in others:
        hid_copy(k).wait_recv()
    for chip in range(z_count):
        across(1, chip).wait_recv()

    contract = (((1,), (1,)), ((), ()))
    for j in range(requests):
        h = hid[:, j].reshape(span, depth)
        thick = lax.dot_general(h, down_all[wanted[j]], contract, preferred_element_type=jnp.float32)
        for s in range(seq_count):
            part[s, j * rows : (j + 1) * rows, :] = thick[s * rows : (s + 1) * rows]
    for k in others:
        part_copy(k).start()
    relay(z_count - 2, 2)

    for k in others:
        up_copy(k).wait_recv()
    for k in others:
        part_copy(k).wait_recv()
    low = part[seq]
    for k in others:
        low = low + part_got[k]
    low = low.astype(jnp.bfloat16)
    cosine = cos_in[...]
    sine = sin_in[...]

    def rotated(u):
        return u * cosine + pltpu.roll(u, rank, 1) * sine

    ups = [up_got[:, j].reshape(rank, up_got.shape[3]) for j in range(requests)]
    for j in range(requests):
        low_q = low[j * rows : (j + 1) * rows, :rank]
        delta_q = jnp.dot(low_q, ups[j][:, :q_width], preferred_element_type=jnp.float32)
        for h in range(head_count):
            cols = slice(h * head_dim, (h + 1) * head_dim)
            u = q_base[j, :, cols].astype(jnp.float32) + delta_q[:, cols]
            queries[j, h * rows : (h + 1) * rows, :] = rotated(u).astype(jnp.bfloat16)

    for chip in range(z_count):
        across(2, chip).wait_recv()
    thin = []
    for j in range(requests):
        h = hid[:, j].reshape(span, depth)
        thin.append(
            lax.dot_general(h, down_end[wanted[j]], contract, preferred_element_type=jnp.float32)
        )
    joined = jnp.concatenate(thin, axis=1)
    for s in range(seq_count):
        part_end[s] = joined[s * rows : (s + 1) * rows]
    for k in others:
        end_copy(k).start()

    for k in others:
        kv_copy(k).wait_recv()
    scale = head_dim ** (-0.5)
    group = 4 * rows

    def extend():
        for k in others:
            end_copy(k).wait_recv()
        low_end = part_end[seq]
        for k in others:
            low_end = low_end + end_got[k]
        low_end = low_end.astype(jnp.bfloat16)
        for j in range(requests):
            low_k = low[j * rows : (j + 1) * rows, rank:]
            low_v = low_end[:, j * rank : (j + 1) * rank]
            up = ups[j]
            delta_k = jnp.dot(low_k, up[:, q_width : q_width + head_dim], preferred_element_type=jnp.float32)
            delta_v = jnp.dot(
                low_v,
                up[:, q_width + head_dim : q_width + 2 * head_dim],
                preferred_element_type=jnp.float32,
            )
            base = kv_base[j].astype(jnp.float32)
            key = rotated(base[:, :head_dim] + delta_k).astype(jnp.bfloat16)
            value = (base[:, head_dim:] + delta_v).astype(jnp.bfloat16)
            fresh = jnp.concatenate([key, value], axis=1)
            new_kv[j] = fresh
            kv_new[j, pl.ds(seq * rows, rows), :] = fresh
        for k in others:
            new_copy(k).start()

    for j in range(requests):
        for g in range(head_count * rows // group):
            at = slice(g * group, (g + 1) * group)
            scores = (
                lax.dot_general(
                    queries[j, at, :],
                    kv_all[j, :, :head_dim],
                    contract,
                    preferred_element_type=jnp.float32,
                )
                * scale
            )
            m = jnp.max(scores, axis=1, keepdims=True)
            w = jnp.exp(scores - m)
            top[j, at, :] = jnp.broadcast_to(m, (group, head_dim))
            total[j, at, :] = jnp.broadcast_to(jnp.sum(w, axis=1, keepdims=True), (group, head_dim))
            acc[j, at, :] = jnp.dot(
                w.astype(jnp.bfloat16), kv_all[j, :, head_dim:], preferred_element_type=jnp.float32
            )
        if j == 0:
            extend()

    for k in others:
        new_copy(k).wait_recv()
    token = lax.rem(lax.broadcasted_iota(jnp.int32, (group, span), 0), rows) + seq * rows
    visible = lax.broadcasted_iota(jnp.int32, (group, span), 1) <= token
    for j in range(requests):
        heads = []
        for g in range(head_count * rows // group):
            at = slice(g * group, (g + 1) * group)
            scores = (
                lax.dot_general(
                    queries[j, at, :],
                    kv_new[j, :, :head_dim],
                    contract,
                    preferred_element_type=jnp.float32,
                )
                * scale
            )
            scores = jnp.where(visible, scores, masked_score)
            old = top[j, at, :]
            m = jnp.maximum(old, jnp.max(scores, axis=1, keepdims=True))
            w = jnp.exp(scores - m[:, :1])
            factor = jnp.exp(old - m)
            denom = total[j, at, :] * factor + jnp.sum(w, axis=1, keepdims=True)
            mixed = acc[j, at, :] * factor + jnp.dot(
                w.astype(jnp.bfloat16), kv_new[j, :, head_dim:], preferred_element_type=jnp.float32
            )
            mixed = (mixed / denom).astype(jnp.bfloat16)
            for i in range(group // rows):
                heads.append(mixed[i * rows : (i + 1) * rows])
        attention = jnp.concatenate(heads, axis=1)
        attn_out[j] = attention
        o_low[j] = lax.dot_general(
            attention, ups[j][:, q_width + 2 * head_dim :], contract, preferred_element_type=jnp.float32
        )

    for k in others:
        for copy in (hid_copy(k), kv_copy(k), up_copy(k), part_copy(k), end_copy(k), new_copy(k)):
            copy.wait_send()
    for kind in range(3):
        for chip in range(z_count):
            across(kind, chip).wait_send()
        for way in range(2):
            for step in range(z_count - 1):

                @pl.when(can_send(way, step))
                def _(way=way, step=step, kind=kind):
                    along(way, step, kind, passed(way, step)).wait_send()


def fused(
    hidden_in, q_base, kv_base, cache_kv, req_adapter, slot_of_adapter, down_panels, up_panels
):
    requests, rows, _ = hidden_in.shape
    head_dim = kv_base.shape[2] // 2
    q_width = q_base.shape[2]
    pre_rows = cache_kv.shape[1]
    seq_count = lax.axis_size("seq")
    req_count = lax.axis_size("req")
    depth = down_panels.shape[1]
    rank_rows, up_width = up_panels.shape[1:]
    z_count = req_count // 2
    half_dim = head_dim // 2
    panel = down_panels[0].T
    positions = (
        pre_rows * seq_count
        + lax.axis_index("seq") * rows
        + jnp.arange(rows, dtype=jnp.int32)
    )
    inverse = 500000.0 ** (-jnp.arange(half_dim, dtype=jnp.float32) / half_dim)
    angles = positions.astype(jnp.float32)[:, None] * inverse[None, :]
    cosine = jnp.cos(angles)
    sine = jnp.sin(angles)
    cosine = jnp.concatenate([cosine, cosine], axis=1)
    sine = jnp.concatenate([-sine, sine], axis=1)
    span = seq_count * rows
    q_rows = q_width // head_dim * rows
    bf16, f32 = jnp.bfloat16, jnp.float32
    dma = pltpu.SemaphoreType.DMA
    smem = pl.BlockSpec(memory_space=pltpu.SMEM)
    vmem = pl.BlockSpec(memory_space=pltpu.VMEM)
    anywhere = pl.BlockSpec(memory_space=pltpu.HBM)
    return pl.pallas_call(
        functools.partial(attend_kernel, z_count),
        out_shape=(
            jax.ShapeDtypeStruct((requests, rows, q_width), bf16),
            jax.ShapeDtypeStruct((requests, rows, half_dim), f32),
            jax.ShapeDtypeStruct((requests, rows, 2 * head_dim), bf16),
        ),
        in_specs=[smem, smem, anywhere, anywhere, anywhere, anywhere, vmem, vmem, vmem, vmem],
        out_specs=(vmem, vmem, vmem),
        scratch_shapes=[
            pltpu.VMEM((seq_count, requests, rows, depth), bf16),
            pltpu.VMEM((req_count, head_dim, depth), bf16),
            pltpu.VMEM((req_count, half_dim, depth), bf16),
            pltpu.VMEM((req_count, rank_rows, up_width), bf16),
            pltpu.VMEM((requests, rank_rows, up_width), bf16),
            pltpu.VMEM((seq_count, requests, rank_rows, up_width), bf16),
            pltpu.VMEM((requests, seq_count * pre_rows, 2 * head_dim), bf16),
            pltpu.VMEM((requests, span, 2 * head_dim), bf16),
            pltpu.VMEM((seq_count, requests * rows, head_dim), f32),
            pltpu.VMEM((seq_count, requests * rows, head_dim), f32),
            pltpu.VMEM((seq_count, rows, head_dim), f32),
            pltpu.VMEM((seq_count, rows, head_dim), f32),
            pltpu.VMEM((requests, q_rows, head_dim), bf16),
            pltpu.VMEM((requests, q_rows, head_dim), f32),
            pltpu.VMEM((requests, q_rows, head_dim), f32),
            pltpu.VMEM((requests, q_rows, head_dim), f32),
            dma((5,)),
        ]
        + [dma((seq_count,))] * 12
        + [dma((2, z_count - 1, 3))] * 2
        + [dma((3, z_count))] * 2,
        compiler_params=pltpu.CompilerParams(
            collective_id=0, has_side_effects=True, vmem_limit_bytes=48 * 1024 * 1024
        ),
    )(
        req_adapter,
        slot_of_adapter,
        hidden_in,
        panel,
        up_panels[0],
        cache_kv,
        q_base,
        kv_base,
        cosine,
        sine,
    )


def fits(mesh):
    return mesh.shape["req"] % 2 == 0 and mesh.shape["seq"] <= 4


def solution(mesh):
    return jax.shard_map(
        fused if fits(mesh) else on_device,
        mesh=mesh,
        in_specs=(
            P("req", "seq", None),
            P("req", "seq", None),
            P("req", "seq", None),
            P("req", "seq", None),
            P(),
            P(),
            P("req", "seq", None),
            P("req", "seq", None),
        ),
        out_specs=(P("req", "seq", None), P("req", "seq", None), P("req", "seq", None)),
        check_vma=False,
    )
```
